32 devices in a mesh: groups: 2 (over y), expert: 4 (over x, core), replica: 4 (over z).
Axes of the slice: x: 2, y: 2, z: 4, core: 2. Of those that a mesh axis runs over, the one named last changes fastest.
Arguments:
- tokens: bfloat16 [768, 7168], P(('groups', 'expert'), 'replica'), parts along dimension 0, may hold values from -6 to 6
- expert_ids: int32 [768, 2], P(('groups', 'expert')), parts along dimension 0, may hold values from 0 to 3, all different within a row; in each aligned block of 96 rows (0 to 95, 96 to 191, ...) at most 60 rows name the same one
- affinity: float32 [768, 2], P(('groups', 'expert')), parts along dimension 0, may hold values from 0.05 to 1
- gate_up: bfloat16 [4, 7168, 2, 2048], P('expert', 'replica'), may hold values from -0.0625 to 0.0625
- down_proj: bfloat16 [4, 2048, 7168], P('expert', None, 'replica'), may hold values from -0.125 to 0.125
Outputs:
- mixed: bfloat16 [768, 7168], P(('groups', 'expert'), 'replica'), parts along dimension 0
The draws below stay inside these ranges and needn't reach their ends.
There are 2 independent parts, one for each index of `groups`. The reference program is written for one: setup_inputs(seed, part) draws one part's arguments, and reference() takes and returns one part's arrays. A program takes and returns all parts, laid end to end along the dimension named above; an argument that names none is the same for every part. Nothing has to cross between parts.
Inputs may be any that keep to these rules, and one draw needn't show every extreme that they name: `expert_ids`: each row names 2 different experts. Within each aligned block of 96 rows no expert is named by more than 60 rows, a bound that some block reaches.
All inputs are finite; a program needn't handle non-finite values.
Results may differ from the reference program's by a relative error of at most 0.023.
Values may be sent and summed in bfloat16 or wider, within the bound.
No kernel may reach another device: no remote copies, remote signals or barrier semaphores. Data moves between devices by JAX's collectives and lax.ppermute only.
A program may use at most 128 MiB of HBM per device.

```python
import math
import jax
import jax.numpy as jnp
import numpy as np
from jax import lax

D = 7168
FF = 2048
TOK_DEV = 96
EXPERTS = 4
TOP = 2
CAP = 60
TOKENS = 384
N_EXPERT = 4
N_REPLICA = 4


def shard_levels(own_key, extent, shards, low, top_value):
    level, own = 1.0, jax.random.fold_in(own_key, 6)
    for dim, shards_of in shards:
        draws = jnp.exp(jax.random.uniform(jax.random.fold_in(own, dim), (shards_of,), jnp.float32, low / len(shards), top_value / len(shards)))
        level = level * jnp.repeat(draws, extent[dim] // shards_of).reshape([-1 if axis == dim else 1 for axis in range(len(extent))])
    return level


def deal_out(rng, own, number, rows, amount, top, limit, skew):
    order = jax.random.permutation(rng, amount)
    heavy_load, usual = shares(amount, rows * top, limit, skew, True), shares(amount, rows * top, limit, skew, False)
    places = jnp.arange(amount)

    def named(lengths, rotation):
        used = int((lengths > 0).sum())
        fixed = max(1, used // 4)
        shifted = fixed + (places - fixed + rotation * (used - fixed)) % max(1, amount - fixed)
        return jnp.zeros((amount,), jnp.int32).at[order[jnp.where(places < fixed, places, shifted)]].set(jnp.asarray(lengths, jnp.int32))

    lengths = jnp.where(number % 4 == 0, named(heavy_load, number // 4), named(usual, number - number // 4 - 1))
    mixed = jax.random.permutation(jax.random.fold_in(own, 3), amount)
    donor, sink = mixed[0:amount // 2 * 2:2], mixed[1:amount // 2 * 2:2]
    room = jnp.minimum(lengths[donor] - 1, limit - lengths[sink]) // 2
    room = jnp.where((donor == order[0]) | (sink == order[0]) | (lengths[sink] == 0), 0, jnp.maximum(room, 0))
    shifted = jax.random.randint(jax.random.fold_in(own, 4), (amount // 2,), 0, 1 << 20) % (room + 1)
    lengths = lengths.at[donor].add(-shifted).at[sink].add(shifted)
    members = jnp.searchsorted(jnp.cumsum(lengths), jnp.arange(rows * top), side="right").astype(jnp.int32)
    listing = members.reshape(top, rows).T
    listing = listing[jax.random.permutation(jax.random.fold_in(own, 1), rows)]
    rotation = jax.random.randint(jax.random.fold_in(own, 2), (rows, 1), 0, top)
    return jnp.take_along_axis(listing, (jnp.arange(top)[None, :] + rotation) % top, axis=1)


def shares(count, total, limit, slope, full):
    weights = [(1 << 20) // math.isqrt(grade ** slope) + 1 for grade in range(1, count + 1)]
    largest = limit if full else min(limit, max(-(-total // count), total * weights[0] // sum(weights)))
    least = 1 if total - largest >= count - 1 else 0
    counts, surplus = [largest] + [least] * (count - 1), total - largest - least * (count - 1)
    while surplus > 0:
        movable = [i for i in range(1, count) if counts[i] < largest] or [i for i in range(1, count) if counts[i] < limit]
        pool, left = sum([weights[i] for i in movable]), surplus
        for i in movable:
            extra = min(limit - counts[i], max(1, left * weights[i] // pool), surplus)
            counts[i] = counts[i] + extra
            surplus = surplus - extra
    return np.array(counts)


def noise(key, shape, spread, most, cuts=(), kind=jnp.bfloat16):
    entries = spread * jax.random.normal(key, shape, jnp.float32)
    if cuts:
        entries = entries * shard_levels(key, shape, cuts, -0.22, 0.18)
    return jnp.clip(entries, -most, most).astype(kind)


def setup_inputs(seed: int = 0, part: int = 0) -> dict:
    keys = jax.random.split(jax.random.key(seed), 6)
    part_splits = jax.random.split(jax.random.fold_in(keys[5], part), 6)
    tokens = noise(part_splits[0], (TOKENS, D), 1.0, 6.0, ((0, 4), (1, 4)))
    expert_ids_keys = jax.random.split(jax.random.fold_in(part_splits[1], 1), TOKENS // TOK_DEV)
    expert_ids_turns = jax.random.permutation(jax.random.fold_in(part_splits[1], 3), TOKENS // TOK_DEV)
    expert_ids = jax.vmap(lambda own, number: deal_out(jax.random.fold_in(part_splits[1], 2), own, number, TOK_DEV, EXPERTS, TOP, CAP, 2))(expert_ids_keys, expert_ids_turns).reshape((TOKENS, TOP))
    affinity = jnp.clip(0.05 + 0.95 * jax.random.uniform(part_splits[2], (TOKENS, TOP), jnp.float32) ** shard_levels(part_splits[2], (TOKENS, TOP), ((0, 4),), -0.2, 0.2), 0.05, 1.0)
    gate_up = noise(keys[3], (EXPERTS, D, 2, FF), D ** -0.5, 0.0625, ((0, 4), (1, 4)))
    down_proj = noise(keys[4], (EXPERTS, FF, D), FF ** -0.5, 0.125, ((0, 4), (2, 4)))
    return dict(tokens=tokens, expert_ids=expert_ids, affinity=affinity, gate_up=gate_up, down_proj=down_proj)


def reference(tokens, expert_ids, affinity, gate_up, down_proj):
    row_count = tokens.shape[0]
    slot_total = N_EXPERT * CAP
    width_slice = D // N_REPLICA
    weights = 2.5 * affinity / jnp.sum(affinity, axis=1, keepdims=True)
    token_index = jnp.arange(row_count, dtype=jnp.int32)
    padded = jnp.concatenate([tokens, jnp.zeros((1, D), tokens.dtype)], axis=0)

    def one_expert(running, expert_id):
        routed_mask = expert_ids == expert_id
        routed = jnp.any(routed_mask, axis=1)
        row_weight = jnp.sum(jnp.where(routed_mask, weights, jnp.zeros_like(weights)), axis=1)
        position = jnp.cumsum(routed.astype(jnp.int32)) - 1
        target = jnp.where(routed, position, slot_total).astype(jnp.int32)
        source = jnp.full((slot_total,), row_count, jnp.int32).at[target].set(token_index, mode="drop")
        chosen = padded[source]
        weight_pair = lax.dynamic_index_in_dim(gate_up, expert_id, 0, keepdims=False)
        sliced = chosen.astype(jnp.float32).reshape(slot_total, N_REPLICA, width_slice)
        weight_sliced = weight_pair.astype(jnp.float32).reshape(N_REPLICA, width_slice, 2 * FF)
        partials = jnp.einsum("rsd,sdf->srf", sliced, weight_sliced, precision=lax.Precision.HIGHEST)
        rounded = lax.optimization_barrier(partials.astype(jnp.bfloat16))
        pre_act = jnp.sum(rounded.astype(jnp.float32), axis=0).reshape(slot_total, 2, FF)
        hidden = (jax.nn.silu(pre_act[:, 0]) * pre_act[:, 1]).astype(jnp.bfloat16)
        down_rows = lax.dynamic_index_in_dim(down_proj, expert_id, 0, keepdims=False)
        expert_rows = jnp.dot(hidden, down_rows, preferred_element_type=jnp.float32).astype(jnp.bfloat16)
        slot_weight = jnp.concatenate([row_weight, jnp.zeros((1,), row_weight.dtype)])[source]
        running = running.at[source].add(slot_weight[:, None] * expert_rows.astype(slot_weight.dtype))
        return running, source

    initial = jnp.zeros((row_count + 1, D), jnp.float32)
    mixed, ignored = lax.scan(one_expert, initial, jnp.arange(EXPERTS, dtype=jnp.int32))
    return mixed[:row_count].astype(jnp.bfloat16)
```

```python
import jax
import jax.numpy as jnp
from jax import lax
from jax.experimental import pallas as pl
from jax.experimental.pallas import tpu as pltpu
from jax.sharding import PartitionSpec as P

F32, BF16, I32 = jnp.float32, jnp.bfloat16, jnp.int32


def routing(me, ids, experts):
    choices, rows = ids.shape
    label = me ^ lax.broadcasted_iota(I32, (experts, rows), 0)
    chosen = jnp.zeros((experts, rows), F32)
    for k in range(choices):
        chosen = chosen + (ids[k : k + 1] == label).astype(F32)
    earlier = lax.broadcasted_iota(I32, (rows, rows), 0) < lax.broadcasted_iota(I32, (rows, rows), 1)
    rank = jnp.dot(chosen.astype(BF16), earlier.astype(F32).astype(BF16), preferred_element_type=F32)
    slot = jnp.where(chosen > 0, rank.astype(I32), -1)
    return label, slot


def one_hot(slot_row, capacity):
    rows = slot_row.shape[1]
    return slot_row == lax.broadcasted_iota(I32, (capacity, rows), 0)


def dispatch_body(me_ref, ids_ref, tokens_ref, *out_refs):
    experts, capacity = len(out_refs), out_refs[0].shape[0]
    _, slot = routing(me_ref[0], ids_ref[...], experts)
    tokens = tokens_ref[...]
    for s, out in enumerate(out_refs):
        pick = one_hot(slot[s : s + 1], capacity).astype(F32).astype(BF16)
        out[...] = jnp.dot(pick, tokens, preferred_element_type=F32).astype(BF16)


def combine_body(me_ref, ids_ref, affinity_ref, *refs):
    *in_refs, out = refs
    experts, capacity = len(in_refs), in_refs[0].shape[0]
    ids, affinity = ids_ref[...], affinity_ref[...]
    label, slot = routing(me_ref[0], ids, experts)
    weights = 2.5 * affinity / jnp.sum(affinity, axis=0, keepdims=True)
    per_expert = jnp.zeros(label.shape, F32)
    for k in range(ids.shape[0]):
        per_expert = per_expert + jnp.where(ids[k : k + 1] == label, weights[k : k + 1], 0.0)
    total = jnp.zeros(out.shape, F32)
    for s, ref in enumerate(in_refs):
        rest = jnp.where(one_hot(slot[s : s + 1], capacity), per_expert[s : s + 1], 0.0)
        for _ in range(3):
            part = rest.astype(BF16)
            rest = rest - part.astype(F32)
            total = total + lax.dot_general(
                part, ref[...], (((0,), (0,)), ((), ())), preferred_element_type=F32
            )
    out[...] = total.astype(BF16)


def vmem(count):
    return [pl.BlockSpec(memory_space=pltpu.VMEM)] * count


def edge_pairs(count, parity, right, left):
    pairs = [(p, p + 1) for p in range(count - 1) if p % 2 == parity and right(p)]
    return pairs + [(p + 1, p) for p in range(count - 1) if p % 2 == parity and left(p + 1)]


def per_device(tokens, expert_ids, affinity, gate_up, down_proj):
    experts, replicas = lax.axis_size("expert"), lax.axis_size("replica")
    rows, choices = expert_ids.shape
    capacity = 5 * rows * choices // (4 * experts)
    width = tokens.shape[1]
    hidden_width = down_proj.shape[1]
    block = hidden_width // replicas
    me = lax.axis_index("expert").astype(I32)[None]
    here = lax.axis_index("replica")
    even = here % 2 == 0
    ids = expert_ids.T
    scalar = [pl.BlockSpec(memory_space=pltpu.SMEM)]

    slots = pl.pallas_call(
        dispatch_body,
        out_shape=[jax.ShapeDtypeStruct((capacity, width), BF16)] * experts,
        in_specs=scalar + vmem(2),
        out_specs=vmem(experts),
        name="dispatch",
    )(me, ids, tokens)

    def swap(x, s):
        return lax.ppermute(x, "expert", [(i, i ^ s) for i in range(experts)])

    arrived = [slots[0]] + [swap(slots[s], s) for s in range(1, experts)]
    x = jnp.concatenate(arrived, axis=0)
    weights = gate_up[0].reshape(width, 2 * hidden_width)
    partial = jnp.dot(x, weights, preferred_element_type=F32).astype(BF16)

    def columns(q):
        q = jnp.clip(q, 0, replicas - 1) * block
        g = lax.dynamic_slice(partial, (0, q), (x.shape[0], block))
        u = lax.dynamic_slice(partial, (0, hidden_width + q), (x.shape[0], block))
        return jnp.concatenate([g, u], axis=1).astype(F32)

    def hop(x, parity, right, left):
        pairs = edge_pairs(replicas, parity, right, left)
        return lax.ppermute(x, "replica", pairs) if pairs else jnp.zeros_like(x)

    got_a = got_b = None
    for s in range(1, replicas):
        to_right, to_left = replicas - s + here, here - replicas + s
        send_a = columns(jnp.where(even, to_right, to_left))
        send_b = columns(jnp.where(even, to_left, to_right))
        if s > 1:
            send_a, send_b = send_a + got_b.astype(F32), send_b + got_a.astype(F32)
        right, left = (lambda p: p <= s - 1), (lambda p: p >= replicas - s)
        got_a = hop(send_a.astype(BF16), 0, right, left)
        got_b = hop(send_b.astype(BF16), 1, right, left)
    pre = columns(here) + got_a.astype(F32) + got_b.astype(F32)
    hidden = (jax.nn.silu(pre[:, :block]) * pre[:, block:]).astype(BF16)

    def down(h, q):
        q = jnp.clip(q, 0, replicas - 1) * block
        part = lax.dynamic_slice(down_proj[0], (q, 0), (block, width))
        return jnp.dot(h, part, preferred_element_type=F32)

    result = down(hidden, here)
    send_a = send_b = hidden
    for s in range(1, replicas):
        right, left = (lambda p: p >= s - 1), (lambda p: p <= replicas - s)
        got_a = hop(send_a, 0, right, left)
        got_b = hop(send_b, 1, right, left)
        result = result + down(got_a, jnp.where(even, here + s, here - s))
        result = result + down(got_b, jnp.where(even, here - s, here + s))
        send_a, send_b = got_b, got_a
    back = result.astype(BF16).reshape(experts, capacity, width)
    returned = [back[0]] + [swap(back[s], s) for s in range(1, experts)]

    return pl.pallas_call(
        combine_body,
        out_shape=jax.ShapeDtypeStruct((rows, width), BF16),
        in_specs=scalar + vmem(2 + experts),
        out_specs=vmem(1)[0],
        name="combine",
    )(me, ids, affinity.T, *returned)


def solution(mesh):
    placed = (
        P(("groups", "expert"), "replica"),
        P(("groups", "expert"), None),
        P(("groups", "expert"), None),
        P("expert", "replica", None, None),
        P("expert", None, "replica"),
    )
    return jax.shard_map(
        per_device,
        mesh=mesh,
        in_specs=placed,
        out_specs=P(("groups", "expert"), "replica"),
        check_vma=False,
    )
```

```python
import functools

import jax
import jax.numpy as jnp
from jax import lax
from jax.experimental import pallas as pl
from jax.experimental.pallas import tpu as pltpu
from jax.sharding import PartitionSpec as P

F32, BF16, I32 = jnp.float32, jnp.bfloat16, jnp.int32
LANES = 128
PARTS = 1


def batches(capacity):
    step = -(-capacity // PARTS)
    step = min(capacity, -(-step // 16) * 16) if PARTS > 1 else capacity
    return [(first, min(step, capacity - first)) for first in range(0, capacity, step)]


def block_to_send(here, replicas, step, parity):
    right, left = replicas - step + here, here - replicas + step
    return jnp.clip(jnp.where(here % 2 == parity, right, left), 0, replicas - 1)


def paired(here, replicas, parity):
    other = jnp.where(here % 2 == parity, here + 1, here - 1)
    return (other >= 0) & (other < replicas)


def block_in_order(here, replicas, t):
    return (block_to_send(here, replicas, 1, 0) + t) % replicas


def dispatch_body(me_ref, ids_hbm, tokens_hbm, *refs, experts, runs):
    *out_refs, ids_ref, tokens_ref, done = refs
    ids_copy = pltpu.make_async_copy(ids_hbm, ids_ref, done.at[0])
    tokens_copy = pltpu.make_async_copy(tokens_hbm, tokens_ref, done.at[1])
    ids_copy.start()
    tokens_copy.start()
    ids_copy.wait()
    ids = ids_ref[...]
    choices, rows = ids.shape
    label = me_ref[0] ^ lax.broadcasted_iota(I32, (experts, rows), 0)
    chosen = jnp.zeros((experts, rows), F32)
    for k in range(choices):
        chosen = chosen + (ids[k : k + 1] == label).astype(F32)
    earlier = lax.broadcasted_iota(I32, (rows, rows), 0) < lax.broadcasted_iota(I32, (rows, rows), 1)
    rank = jnp.dot(chosen.astype(BF16), earlier.astype(F32).astype(BF16), preferred_element_type=F32)
    slot = jnp.where(chosen > 0, rank.astype(I32), -1)
    tokens_copy.wait()
    tokens = tokens_ref[...]
    for b, (first, count) in enumerate(runs):
        for s in range(experts):
            pick = slot[s : s + 1] == first + lax.broadcasted_iota(I32, (count, rows), 0)
            pick = pick.astype(F32).astype(BF16)
            out_refs[b * experts + s][...] = jnp.dot(pick, tokens, preferred_element_type=F32).astype(BF16)


def mixing_body(me_ref, ids_ref, affinity_ref, out_ref, *, experts, runs):
    ids, affinity = ids_ref[...], affinity_ref[...]
    rows, choices = ids.shape
    label = me_ref[0] ^ lax.broadcasted_iota(I32, (rows, experts), 1)
    chosen = jnp.zeros((rows, experts), F32)
    for k in range(choices):
        chosen = chosen + (ids[:, k : k + 1] == label).astype(F32)
    earlier = lax.broadcasted_iota(I32, (rows, rows), 1) < lax.broadcasted_iota(I32, (rows, rows), 0)
    rank = jnp.dot(earlier.astype(F32).astype(BF16), chosen.astype(BF16), preferred_element_type=F32)
    weights = 2.5 * affinity / jnp.sum(affinity, axis=1, keepdims=True)
    base = 0
    for first, count in runs:
        padded = -(-count // 16) * 16
        within = rank.astype(I32) - first
        place = base + padded * lax.broadcasted_iota(I32, (rows, experts), 1) + within
        place = jnp.where((chosen > 0) & (within >= 0) & (within < count), place, -1)
        column = base + lax.broadcasted_iota(I32, (rows, experts * padded), 1)
        rest = jnp.zeros(column.shape, F32)
        for k in range(choices):
            mine = ids[:, k : k + 1] == label
            spot = jnp.max(jnp.where(mine, place, -1), axis=1, keepdims=True)
            rest = rest + jnp.where(spot == column, weights[:, k : k + 1], 0.0)
        for i in range(3):
            part = rest.astype(BF16)
            rest = rest - part.astype(F32)
            out_ref[i, :, base : base + experts * padded] = part
        base += experts * padded


def combine_body(mixing_ref, *refs, runs, experts):
    *in_refs, out, gathered = refs
    base = 0
    for b, (first, count) in enumerate(runs):
        padded = -(-count // 16) * 16
        for s in range(experts):
            if padded > count:
                tail = base + padded - 16
                gathered[tail : tail + 16] = jnp.zeros((16, gathered.shape[1]), BF16)
            gathered[base : base + count] = in_refs[b * experts + s][...]
            base += padded
    rows = out.shape[0]
    terms, _, slots = mixing_ref.shape
    picked = jnp.dot(
        mixing_ref[...].reshape(terms * rows, slots), gathered[...], preferred_element_type=F32
    )
    total = picked[:rows]
    for i in range(1, terms):
        total = total + picked[i * rows : (i + 1) * rows]
    out[...] = total.astype(BF16)


def tile_copy(pairs_ref, tile, buffer_ref, at, done):
    return pltpu.make_async_copy(pairs_ref.at[:, tile], buffer_ref.at[at], done.at[at])


def prepare_body(place_ref, *refs, replicas, start):
    pairs_ref, out_ref, buffer_ref, done = refs[-4:]
    blocks, width, columns = out_ref.shape
    per = columns // (2 * LANES)
    pairs_per = per // 2
    steps = blocks * pairs_per
    depth = buffer_ref.shape[0] // 2
    flat = buffer_ref.reshape(2 * depth, 2 * width, LANES)

    def fetch(t):
        q = block_in_order(place_ref[1], replicas, start + t // pairs_per)
        tile = q * per + 2 * (t % pairs_per)
        for i in range(2):
            tile_copy(pairs_ref, tile + i, buffer_ref, 2 * (t % depth) + i, done).start()

    for t in range(min(depth - 1, steps)):
        fetch(t)
    side = 2 * LANES
    row = lax.broadcasted_iota(I32, (side, side), 0)
    column = lax.broadcasted_iota(I32, (side, side), 1)
    sort = (column == 2 * row) | (column == 2 * (row - LANES) + 1)
    sort = sort.astype(F32).astype(BF16)

    def step(t, carry):
        @pl.when(t + depth - 1 < steps)
        def _():
            fetch(t + depth - 1)

        q = t // pairs_per
        gate = pl.multiple_of((t % pairs_per) * side, side)
        up = pl.multiple_of(per * LANES + (t % pairs_per) * side, side)
        at = 2 * (t % depth)
        for i in range(2):
            tile_copy(pairs_ref, 0, buffer_ref, at + i, done).wait()
        for r in range(width // LANES):
            rows = slice(r * side, (r + 1) * side)
            mixed = jnp.concatenate([flat[at, rows], flat[at + 1, rows]], axis=1)
            sorted_rows = jnp.dot(sort, mixed, preferred_element_type=F32).astype(BF16)
            out_ref[q, r * LANES : (r + 1) * LANES, pl.ds(gate, side)] = sorted_rows[:LANES]
            out_ref[q, r * LANES : (r + 1) * LANES, pl.ds(up, side)] = sorted_rows[LANES:]
        return carry

    lax.fori_loop(0, steps, step, 0)


def gather_rows(x_refs, rows_ref):
    count = rows_ref.shape[0] // len(x_refs)
    for s, x in enumerate(x_refs):
        rows_ref[s * count : (s + 1) * count] = x[...]


def columns_of(rows_ref, weights_ref, t, store):
    for c in range(0, weights_ref.shape[2], 2 * LANES):
        part = weights_ref[t, :, c : c + 2 * LANES]
        store(c, jnp.dot(rows_ref[...], part, preferred_element_type=F32).astype(BF16))


def first_body(*refs, experts):
    x_refs, (weights_ref, first_ref, rows_ref) = refs[:experts], refs[experts:]
    gather_rows(x_refs, rows_ref)

    def store(c, value):
        first_ref[:, c : c + 2 * LANES] = value

    columns_of(rows_ref, weights_ref, 0, store)


def rest_body(place_ref, first_ref, *refs, experts):
    x_refs, (early_ref, late_ref, out_ref, second_ref, rows_ref) = refs[:experts], refs[experts:]
    here, blocks = place_ref[1], out_ref.shape[0]
    gather_rows(x_refs, rows_ref)
    out_ref[block_in_order(here, blocks, 0)] = first_ref[...]
    for t in range(1, blocks):
        q = block_in_order(here, blocks, t)

        def store(c, value):
            out_ref[q, :, c : c + 2 * LANES] = value

        early = early_ref.shape[0]
        columns_of(rows_ref, early_ref if t < early else late_ref, t if t < early else t - early, store)
    second_ref[...] = out_ref[block_to_send(here, blocks, 2, 0)]


def add_body(place_ref, partial_ref, got_ref, out_ref, *, step, parity):
    here, replicas = place_ref[1], partial_ref.shape[0]
    own = partial_ref[block_to_send(here, replicas, step, parity)].astype(F32)
    got = jnp.where(paired(here, replicas, 1 - parity), got_ref[...].astype(F32), 0.0)
    out_ref[...] = (own + got).astype(BF16)


def hidden_body(place_ref, partial_ref, *refs, parities):
    *got_refs, out_ref = refs
    here, replicas = place_ref[1], partial_ref.shape[0]
    pre = partial_ref[here].astype(F32)
    for parity, got in zip(parities, got_refs):
        pre = pre + jnp.where(paired(here, replicas, parity), got[...].astype(F32), 0.0)
    block = out_ref.shape[1]
    gate = pre[:, :block]
    out_ref[...] = (gate / (1.0 + jnp.exp(-gate)) * pre[:, block:]).astype(BF16)


def down_body(place_ref, down_ref, *refs, step, parities, own, last, replicas):
    here = place_ref[1]
    block = down_ref.shape[0] // replicas
    known = refs[0]
    got_refs = refs[1 : 1 + len(parities)]
    out_refs = refs[1 + len(parities) :]
    total = out_refs[-1]

    def product(h_ref, q):
        part = down_ref[pl.ds(pl.multiple_of(q * block, block), block)]
        return jnp.dot(h_ref[...], part, preferred_element_type=F32)

    total[...] = product(known, here) if own else known[...]
    for parity, got in zip(parities, got_refs):
        q = jnp.where(here % 2 == parity, here + step, here - step)

        @pl.when((q >= 0) & (q < replicas))
        def _():
            total[...] = total[...] + product(got, q)

    if last:
        count = out_refs[0].shape[0]
        for s, out in enumerate(out_refs[:-1]):
            out[...] = total[s * count : (s + 1) * count].astype(BF16)


def vmem(count):
    return [pl.BlockSpec(memory_space=pltpu.VMEM)] * count


def smem():
    return [pl.BlockSpec(memory_space=pltpu.SMEM)]


def hbm(count):
    return [pl.BlockSpec(memory_space=pltpu.HBM)] * count


def in_hbm(x):
    return pltpu.with_memory_space_constraint(x, pltpu.HBM)


def params(mib):
    return pltpu.CompilerParams(vmem_limit_bytes=mib << 20)


def partner(p, parity):
    return p + 1 if p % 2 == parity else p - 1


def neighbours(experts, count, parity):
    swaps = []
    for e in range(experts):
        for p in range(count):
            q = partner(p, parity)
            other = (e, q) if 0 <= q < count else (e ^ 1, p)
            swaps.append((e * count + p, other[0] * count + other[1]))
    return swaps


def needed(count, parity, right, left):
    edges = [p for p in range(count - 1) if p % 2 == parity]
    return any(right(p) or left(p + 1) for p in edges)


def per_device(tokens, expert_ids, affinity, gate_up, down_proj):
    experts, replicas = lax.axis_size("expert"), lax.axis_size("replica")
    rows, choices = expert_ids.shape
    capacity = 5 * rows * choices // (4 * experts)
    runs = batches(capacity)
    width = tokens.shape[1]
    hidden_width = down_proj.shape[1]
    block = hidden_width // replicas
    me = lax.axis_index("expert").astype(I32)[None]
    here = lax.axis_index("replica").astype(I32)
    place = jnp.stack([me[0], here])

    slots = pl.pallas_call(
        functools.partial(dispatch_body, experts=experts, runs=runs),
        out_shape=[jax.ShapeDtypeStruct((c, width), BF16) for _, c in runs for _ in range(experts)],
        in_specs=smem() + hbm(2),
        out_specs=vmem(experts * len(runs)),
        scratch_shapes=[
            pltpu.VMEM((choices, rows), I32),
            pltpu.VMEM((rows, width), BF16),
            pltpu.SemaphoreType.DMA((2,)),
        ],
        compiler_params=params(8),
        name="dispatch",
    )(place, in_hbm(expert_ids.T), in_hbm(tokens))

    def swap(x, s):
        return lax.ppermute(x, "expert", [(i, i ^ s) for i in range(experts)])

    def hop(x, parity):
        return lax.ppermute(x, ("expert", "replica"), neighbours(experts, replicas, parity))

    arrived = []
    for b in range(len(runs)):
        mine = slots[b * experts : (b + 1) * experts]
        far_first = {s: swap(mine[s], s) for s in range(experts - 1, 0, -1)}
        arrived.append([mine[0]] + [far_first[s] for s in range(1, experts)])

    tiles = hidden_width // LANES
    pairs = gate_up[0].reshape(width, 2, tiles, LANES).transpose(0, 2, 1, 3)
    pairs = in_hbm(pairs)

    def tile_buffers(count):
        return [pltpu.VMEM((count, width, 2, LANES), BF16), pltpu.SemaphoreType.DMA((count,))]

    slots_padded = sum(experts * (-(-c // 16) * 16) for _, c in runs)
    mixing = pl.pallas_call(
        functools.partial(mixing_body, experts=experts, runs=runs),
        out_shape=jax.ShapeDtypeStruct((3, rows, slots_padded), BF16),
        in_specs=smem() + vmem(2),
        out_specs=vmem(1)[0],
        compiler_params=params(8),
        name="mixing",
    )(place, expert_ids, affinity)

    def prepared(start, count, *after):
        return pl.pallas_call(
            functools.partial(prepare_body, replicas=replicas, start=start),
            out_shape=jax.ShapeDtypeStruct((count, width, 2 * block), BF16),
            in_specs=smem() + hbm(1 + len(after)),
            out_specs=vmem(1)[0],
            scratch_shapes=tile_buffers(8),
            compiler_params=params(12),
            name="prepare",
        )(place, *after, pairs)

    early = replicas - replicas // 4
    weights = prepared(0, early)

    def first(x):
        return pl.pallas_call(
            functools.partial(first_body, experts=experts),
            out_shape=jax.ShapeDtypeStruct((experts * x[0].shape[0], 2 * block), BF16),
            in_specs=vmem(experts + 1),
            out_specs=vmem(1)[0],
            scratch_shapes=[pltpu.VMEM((experts * x[0].shape[0], width), BF16)],
            compiler_params=params(8),
            name="first",
        )(*x, weights)

    def reduced(x, ahead, late):
        count = experts * x[0].shape[0]
        sent = jax.ShapeDtypeStruct((count, 2 * block), BF16)
        partial, second = pl.pallas_call(
            functools.partial(rest_body, experts=experts),
            out_shape=[jax.ShapeDtypeStruct((replicas, count, 2 * block), BF16), sent],
            in_specs=smem() + vmem(3 + experts),
            out_specs=vmem(2),
            scratch_shapes=[pltpu.VMEM((count, width), BF16)],
            compiler_params=params(8),
            name="rest",
        )(place, ahead, *x, weights, late)

        def added(step, parity, got):
            return pl.pallas_call(
                functools.partial(add_body, step=step, parity=parity),
                out_shape=sent,
                in_specs=smem() + vmem(2),
                out_specs=vmem(1)[0],
                compiler_params=params(4),
                name="add",
            )(place, partial, got)

        got = [None, None]
        for s in range(1, replicas):
            right, left = (lambda p: p <= s - 1), (lambda p: p >= replicas - s)
            came = list(got)
            for parity in range(2):
                if not needed(replicas, parity, right, left):
                    continue
                if came[1 - parity] is not None:
                    send = added(s, parity, came[1 - parity])
                elif parity == 0 and s <= 2:
                    send = (ahead, second)[s - 1]
                else:
                    q = block_to_send(here, replicas, s, parity)
                    send = lax.dynamic_index_in_dim(partial, q, 0, keepdims=False)
                got[parity] = hop(send, parity)
        parities = [parity for parity in range(2) if got[parity] is not None]
        return pl.pallas_call(
            functools.partial(hidden_body, parities=parities),
            out_shape=jax.ShapeDtypeStruct((count, block), BF16),
            in_specs=smem() + vmem(1 + len(parities)),
            out_specs=vmem(1)[0],
            compiler_params=params(4),
            name="hidden",
        )(place, partial, *[got[parity] for parity in parities])

    def projected(hidden):
        count = hidden.shape[0]
        send, known = [hidden, hidden], hidden
        for s in range(1, replicas):
            right, left = (lambda p: p >= s - 1), (lambda p: p <= replicas - s)
            got = [None, None]
            for parity in range(2):
                if needed(replicas, parity, right, left):
                    got[parity] = hop(send[parity], parity)
            parities = [parity for parity in range(2) if got[parity] is not None]
            last = s == replicas - 1
            back = [jax.ShapeDtypeStruct((count // experts, width), BF16)] * (experts if last else 0)
            *back, known = pl.pallas_call(
                functools.partial(
                    down_body, step=s, parities=parities, own=s == 1, last=last, replicas=replicas
                ),
                out_shape=[*back, jax.ShapeDtypeStruct((count, width), F32)],
                in_specs=smem() + vmem(2 + len(parities)),
                out_specs=vmem(len(back) + 1),
                input_output_aliases={} if s == 1 else {2: len(back)},
                compiler_params=params(8),
                name="down",
            )(place, down_proj[0], known, *[got[parity] for parity in parities])
            send = got[::-1]
        far_first = {s: swap(back[s], s) for s in range(experts - 1, 0, -1)}
        return [back[0]] + [far_first[s] for s in range(1, experts)]

    ahead = [first(x) for x in arrived]
    late = prepared(early, replicas - early, in_hbm(ahead[0]))
    hidden = [reduced(x, a, late) for x, a in zip(arrived, ahead)]
    returned = [r for h in hidden for r in projected(h)]
    return pl.pallas_call(
        functools.partial(combine_body, runs=runs, experts=experts),
        out_shape=jax.ShapeDtypeStruct((rows, width), BF16),
        in_specs=vmem(1 + len(returned)),
        out_specs=vmem(1)[0],
        scratch_shapes=[pltpu.VMEM((slots_padded, width), BF16)],
        compiler_params=params(16),
        name="combine",
    )(mixing, *returned)


def solution(mesh):
    placed = (
        P(("groups", "expert"), "replica"),
        P(("groups", "expert"), None),
        P(("groups", "expert"), None),
        P("expert", "replica", None, None),
        P("expert", None, "replica"),
    )
    return jax.shard_map(
        per_device,
        mesh=mesh,
        in_specs=placed,
        out_specs=P(("groups", "expert"), "replica"),
        check_vma=False,
    )
```
